32 devices in a mesh: seq: 4 (over z), head: 4 (over y, x), batch: 2 (over core).
Axes of the slice: x: 2, y: 2, z: 4, core: 2. Of those that a mesh axis runs over, the one named last changes fastest.
Arguments:
- hidden_in: float32 [2, 512, 768], P('batch', 'seq'), may hold values from -6 to 6
- cotangent: float32 [2, 512, 768], P('batch', 'seq'), may hold values from -6 to 6
- norm_gain: float32 [2, 768], replicated, may hold values from 0.5 to 1.5
- gate_proj: bfloat16 [2, 768, 1536], P(None, None, 'head'), may hold values from -0.21875 to 0.21875
- value_proj: bfloat16 [2, 768, 1536], P(None, None, 'head'), may hold values from -0.21875 to 0.21875
- shared_proj: bfloat16 [2, 768, 256], replicated, may hold values from -0.21875 to 0.21875
- step_proj: bfloat16 [2, 768, 24], P(None, None, 'head'), may hold values from -0.21875 to 0.21875
- conv_value: float32 [2, 4, 1536], P(None, None, 'head'), may hold values from -3 to 3
- conv_value_bias: float32 [2, 1536], P(None, 'head'), may hold values from -3 to 3
- conv_shared: float32 [2, 4, 256], replicated, may hold values from -3 to 3
- conv_shared_bias: float32 [2, 256], replicated, may hold values from -3 to 3
- step_bias: float32 [2, 24], P(None, 'head'), may hold values from -14 to -4
- decay_log: float32 [2, 24], P(None, 'head'), may hold values from -1 to 2
- skip_scale: float32 [2, 24], P(None, 'head'), may hold values from 0.5 to 2
- gate_gain: float32 [2, 1536], P(None, 'head'), may hold values from 0.5 to 1.5
- out_proj: bfloat16 [2, 1536, 768], P(None, 'head'), may hold values from -0.15625 to 0.15625
Outputs:
- hidden_out: float32 [2, 512, 768], P('batch', 'seq')
- hidden_grad: float32 [2, 512, 768], P('batch', 'seq')
- grad_norm_gain: float32 [2, 768], replicated
- grad_gate_proj: float32 [2, 768, 1536], P(None, ('seq', 'batch'), 'head')
- grad_value_proj: float32 [2, 768, 1536], P(None, ('seq', 'batch'), 'head')
- grad_shared_proj: float32 [2, 768, 256], P(None, ('seq', 'batch'))
- grad_step_proj: float32 [2, 768, 24], P(None, ('seq', 'batch'), 'head')
- grad_conv_value: float32 [2, 4, 1536], P(None, None, 'head')
- grad_conv_value_bias: float32 [2, 1536], P(None, 'head')
- grad_conv_shared: float32 [2, 4, 256], replicated
- grad_conv_shared_bias: float32 [2, 256], replicated
- grad_step_bias: float32 [2, 24], P(None, 'head')
- grad_decay_log: float32 [2, 24], P(None, 'head')
- grad_skip_scale: float32 [2, 24], P(None, 'head')
- grad_gate_gain: float32 [2, 1536], P(None, 'head')
- grad_out_proj: float32 [2, 1536, 768], P(None, 'head', ('seq', 'batch'))
The draws below stay inside these ranges and needn't reach their ends.
All inputs are finite; a program needn't handle non-finite values.
Results may differ from the reference program's by a relative error of at most 0.012.
Values sent between devices are 32-bit elements; how exact they have to be, the bound alone decides.
A program may use at most 128 MiB of HBM per device.

```python
import jax
import jax.numpy as jnp
from jax import lax

D = 768
HEADS = 24
NSTATE = 128
CONV = 4
GROUP = 128
LAYERS = 2
INNER = 1536
SEQS = 2
LENGTH = 512


def steps_of(stream_key, dims, cuts, smallest, largest):
    loudness, own = 1.0, jax.random.fold_in(stream_key, 6)
    for axis_at, shards_of in cuts:
        heights = jnp.exp(jax.random.uniform(jax.random.fold_in(own, axis_at), (shards_of,), jnp.float32, smallest / len(cuts), largest / len(cuts)))
        loudness = loudness * jnp.repeat(heights, dims[axis_at] // shards_of).reshape([-1 if axis == axis_at else 1 for axis in range(len(dims))])
    return loudness


def gaussian(own_key, dims, spread, most, split=(), held_as=jnp.bfloat16):
    array = jax.random.normal(own_key, dims, jnp.float32) * spread
    if len(split) > 0:
        array = steps_of(own_key, dims, split, -0.22, 0.18) * array
    return jnp.clip(array, min=-most, max=most).astype(held_as)


def setup_inputs(seed: int = 0) -> dict:
    keys = jax.random.split(jax.random.key(seed), 17)
    hidden_in = gaussian(keys[0], (SEQS, LENGTH, D), 1.0, 6.0, ((0, 2), (1, 4)), jnp.float32)
    cotangent = gaussian(keys[1], (SEQS, LENGTH, D), 1.0, 6.0, ((0, 2), (1, 4)), jnp.float32)
    norm_gain = jnp.clip(1.0 + 0.1 * jax.random.normal(keys[2], (LAYERS, D), jnp.float32), 0.5, 1.5)
    gate_proj = gaussian(keys[3], (LAYERS, D, INNER), D ** -0.5, 0.21875, ((2, 4),))
    value_proj = gaussian(keys[4], (LAYERS, D, INNER), D ** -0.5, 0.21875, ((2, 4),))
    shared_proj = gaussian(keys[5], (LAYERS, D, 2 * NSTATE), D ** -0.5, 0.21875)
    step_proj = gaussian(keys[6], (LAYERS, D, HEADS), D ** -0.5, 0.21875, ((2, 4),))
    conv_value = gaussian(keys[7], (LAYERS, CONV, INNER), CONV ** -0.5, 3.0, ((2, 4),), jnp.float32)
    conv_value_bias = gaussian(keys[8], (LAYERS, INNER), 0.5, 3.0, ((1, 4),), jnp.float32)
    conv_shared = gaussian(keys[9], (LAYERS, CONV, 2 * NSTATE), CONV ** -0.5, 3.0, (), jnp.float32)
    conv_shared_bias = gaussian(keys[10], (LAYERS, 2 * NSTATE), 0.5, 3.0, (), jnp.float32)
    step_bias = jnp.clip(-14.0 + 10.0 * jax.random.uniform(keys[11], (LAYERS, HEADS), jnp.float32) ** steps_of(keys[11], (LAYERS, HEADS), ((1, 4),), -0.2, 0.2), -14.0, -4.0)
    decay_log = jnp.clip(-1.0 + 3.0 * jax.random.uniform(keys[12], (LAYERS, HEADS), jnp.float32) ** steps_of(keys[12], (LAYERS, HEADS), ((1, 4),), -0.2, 0.2), -1.0, 2.0)
    skip_scale = jnp.clip(0.5 + 1.5 * jax.random.uniform(keys[13], (LAYERS, HEADS), jnp.float32) ** steps_of(keys[13], (LAYERS, HEADS), ((1, 4),), -0.2, 0.2), 0.5, 2.0)
    gate_gain = jnp.clip(1.0 + 0.1 * jax.random.normal(keys[14], (LAYERS, INNER), jnp.float32), 0.5, 1.5)
    out_proj = gaussian(keys[15], (LAYERS, INNER, D), INNER ** -0.5, 0.15625, ((1, 4),))
    return dict(hidden_in=hidden_in, cotangent=cotangent, norm_gain=norm_gain, gate_proj=gate_proj, value_proj=value_proj, shared_proj=shared_proj, step_proj=step_proj, conv_value=conv_value, conv_value_bias=conv_value_bias, conv_shared=conv_shared, conv_shared_bias=conv_shared_bias, step_bias=step_bias, decay_log=decay_log, skip_scale=skip_scale, gate_gain=gate_gain, out_proj=out_proj)


epsilon = 1e-05
highest = lax.Precision.HIGHEST

def silu_slope(argument):
    sigmoid_value = jax.nn.sigmoid(argument)
    return sigmoid_value * (1.0 + argument * (1.0 - sigmoid_value))

def blocked(tensor, head_count):
    row_count = tensor.shape[0]
    return tensor.reshape(row_count // GROUP, GROUP, head_count, tensor.shape[1] // head_count)

def norm_input(hidden, norm_gain):
    return hidden * lax.rsqrt(lax.optimization_barrier(jnp.mean(hidden * hidden, axis=-1, keepdims=True)) + epsilon) * norm_gain

def ssd_front(ext_value, ext_shared, conv_value, conv_value_bias, conv_shared, conv_shared_bias, step_raw, step_bias, decay_log):
    row_count, head_count = step_raw.shape
    value_conv = conv_value_bias + jnp.zeros((row_count, ext_value.shape[1]), jnp.float32)
    shared_conv = conv_shared_bias + jnp.zeros((row_count, ext_shared.shape[1]), jnp.float32)
    for k in range(conv_value.shape[0]):
        value_conv = value_conv + conv_value[k] * ext_value[k:k + row_count]
        shared_conv = shared_conv + conv_shared[k] * ext_shared[k:k + row_count]
    values_act = jax.nn.silu(value_conv)
    shared_act = jax.nn.silu(shared_conv)
    state_width = shared_act.shape[1] // 2
    b_mat = shared_act[:, :state_width]
    c_mat = shared_act[:, state_width:]
    step_size = jax.nn.softplus(step_raw + step_bias)
    rate_values = -jnp.exp(decay_log) * step_size
    block_count = row_count // GROUP
    value_blocks = blocked(values_act, head_count)
    b_blocks = b_mat.reshape(block_count, GROUP, state_width)
    step_blocks = step_size.reshape(block_count, GROUP, head_count)
    cum_rates = jnp.cumsum(rate_values.reshape(block_count, GROUP, head_count), axis=1)
    to_end = jnp.exp(cum_rates[:, -1:, :] - cum_rates)
    weighted = value_blocks * (to_end * step_blocks)[..., None]
    summary = jnp.einsum('clhp,cln->chpn', weighted, b_blocks, precision=highest)
    block_decay = jnp.exp(cum_rates[:, -1, :])

    def fold_block(running, element):
        end_state, decay_total = running
        piece_state, piece_decay = element
        return ((piece_decay[:, None, None] * end_state + piece_state, decay_total * piece_decay), None)
    start_pair = (jnp.zeros(summary.shape[1:], jnp.float32), jnp.ones((head_count,), jnp.float32))
    (end_state, decay_total), _ = lax.scan(fold_block, start_pair, (summary, block_decay))
    return (values_act, b_mat, c_mat, step_size, rate_values, summary, block_decay, end_state, decay_total)

def ssd_output(values_act, b_mat, c_mat, step_size, rate_values, skip_scale, summary, block_decay, start_state):
    row_count, head_count = step_size.shape
    block_count = row_count // GROUP
    state_width = b_mat.shape[1]
    value_blocks = blocked(values_act, head_count)
    b_blocks = b_mat.reshape(block_count, GROUP, state_width)
    c_blocks = c_mat.reshape(block_count, GROUP, state_width)
    step_heads = jnp.transpose(step_size.reshape(block_count, GROUP, head_count), (0, 2, 1))
    cum_rates = jnp.cumsum(jnp.transpose(rate_values.reshape(block_count, GROUP, head_count), (0, 2, 1)), axis=2)

    def advance(running, element):
        piece_state, piece_decay = element
        return (piece_decay[:, None, None] * running + piece_state, running)
    _, starts = lax.scan(advance, start_state, (summary, block_decay))
    scores = jnp.einsum('ctn,csn->cts', c_blocks, b_blocks, precision=highest)
    positions = jnp.arange(GROUP)
    causal = positions[:, None] >= positions[None, :]
    gap = cum_rates[:, :, :, None] - cum_rates[:, :, None, :]
    weights = jnp.where(causal, jnp.exp(jnp.where(causal, gap, 0.0)), 0.0)
    mixing = scores[:, None, :, :] * weights * step_heads[:, :, None, :]
    within_out = jnp.einsum('chts,cshp->cthp', mixing, value_blocks, precision=highest)
    carried = jnp.einsum('ctn,chpn->cthp', c_blocks, starts, precision=highest) * jnp.exp(jnp.transpose(cum_rates, (0, 2, 1)))[..., None]
    mixer_out = within_out + carried + skip_scale[None, None, :, None] * value_blocks
    return mixer_out.reshape(row_count, values_act.shape[1])

def layer_slice(stacked, layer_index):
    return tuple((tensor[layer_index] for tensor in stacked))

def layer_forward(hidden, layer_weights):
    norm_gain, gate_proj, value_proj, shared_proj, step_proj, conv_value, conv_value_bias, conv_shared, conv_shared_bias, step_bias, decay_log, skip_scale, gate_gain, out_proj = layer_weights
    normed_b = norm_input(hidden, norm_gain).astype(jnp.bfloat16)
    gate_pre = jnp.dot(normed_b, gate_proj, preferred_element_type=jnp.float32)
    value_pre = jnp.dot(normed_b, value_proj, preferred_element_type=jnp.float32)
    shared_pre = jnp.dot(normed_b, shared_proj, preferred_element_type=jnp.float32)
    step_raw = jnp.dot(normed_b, step_proj, preferred_element_type=jnp.float32)
    rim_rows = conv_value.shape[0] - 1
    ext_value = jnp.concatenate([jnp.zeros((rim_rows, value_pre.shape[1]), jnp.float32), value_pre], axis=0)
    ext_shared = jnp.concatenate([jnp.zeros((rim_rows, shared_pre.shape[1]), jnp.float32), shared_pre], axis=0)
    front_out, front_pull = jax.vjp(ssd_front, ext_value, ext_shared, conv_value, conv_value_bias, conv_shared, conv_shared_bias, step_raw, step_bias, decay_log)
    head_count = step_raw.shape[1]
    start_state = jnp.zeros((head_count, value_pre.shape[1] // head_count, shared_pre.shape[1] // 2), jnp.float32)
    mixer_out, output_pull = jax.vjp(ssd_output, front_out[0], front_out[1], front_out[2], front_out[3], front_out[4], skip_scale, front_out[5], front_out[6], start_state)
    gated_out = mixer_out * jax.nn.silu(gate_pre)
    inv_rms = lax.rsqrt(lax.optimization_barrier(jnp.mean(gated_out * gated_out, axis=-1, keepdims=True)) + epsilon)
    gated_b = (gated_out * inv_rms * gate_gain).astype(jnp.bfloat16)
    branch = jnp.dot(gated_b, out_proj, preferred_element_type=jnp.float32)
    stored = (normed_b, gate_pre, front_out, front_pull, output_pull, mixer_out, gated_out, inv_rms, gated_b, hidden)
    return (hidden + branch, stored)

def layer_backward(d_hidden, stored, layer_weights):
    norm_gain, gate_proj, value_proj, shared_proj, step_proj, conv_value, conv_value_bias, conv_shared, conv_shared_bias, step_bias, decay_log, skip_scale, gate_gain, out_proj = layer_weights
    normed_b, gate_pre, front_out, front_pull, output_pull, mixer_out, gated_out, inv_rms, gated_b, hidden = stored
    branch_b = d_hidden.astype(jnp.bfloat16)
    d_normalized = jnp.dot(branch_b, out_proj.T, preferred_element_type=jnp.float32)
    grad_out = jnp.dot(gated_b.T, branch_b, preferred_element_type=jnp.float32)
    grad_gain_gate = lax.optimization_barrier(jnp.sum(d_normalized * gated_out * inv_rms, axis=0))
    scaled = d_normalized * gate_gain
    inner_dot = lax.optimization_barrier(jnp.mean(scaled * gated_out, axis=-1, keepdims=True))
    d_gated = inv_rms * scaled - gated_out * inv_rms * inv_rms * inv_rms * inner_dot
    d_mixer = d_gated * jax.nn.silu(gate_pre)
    d_gate_pre = d_gated * mixer_out * silu_slope(gate_pre)
    d_values, d_bmat, d_cmat, d_step, d_rates, grad_skip, d_summary, d_decay, d_start = output_pull(d_mixer)
    pulled = front_pull((d_values, d_bmat, d_cmat, d_step, d_rates, d_summary, d_decay, jnp.zeros_like(front_out[7]), jnp.zeros_like(front_out[8])))
    d_ext_value, d_ext_shared, grad_conv_v, grad_conv_vb, grad_conv_s, grad_conv_sb, d_step_raw, grad_step_bias, grad_decay = pulled
    rim_rows = conv_value.shape[0] - 1
    gate_b = d_gate_pre.astype(jnp.bfloat16)
    value_b = d_ext_value[rim_rows:].astype(jnp.bfloat16)
    shared_b = d_ext_shared[rim_rows:].astype(jnp.bfloat16)
    step_b = d_step_raw.astype(jnp.bfloat16)
    d_normed = jnp.dot(gate_b, gate_proj.T, preferred_element_type=jnp.float32)
    d_normed = d_normed + jnp.dot(value_b, value_proj.T, preferred_element_type=jnp.float32)
    d_normed = d_normed + jnp.dot(shared_b, shared_proj.T, preferred_element_type=jnp.float32)
    d_normed = d_normed + jnp.dot(step_b, step_proj.T, preferred_element_type=jnp.float32)
    grad_gate = jnp.dot(normed_b.T, gate_b, preferred_element_type=jnp.float32)
    grad_value = jnp.dot(normed_b.T, value_b, preferred_element_type=jnp.float32)
    grad_shared = jnp.dot(normed_b.T, shared_b, preferred_element_type=jnp.float32)
    grad_step = jnp.dot(normed_b.T, step_b, preferred_element_type=jnp.float32)
    _, norm_pull = jax.vjp(norm_input, hidden, norm_gain)
    d_input, grad_norm = norm_pull(d_normed)
    return (d_hidden + d_input, (grad_norm, grad_gate, grad_value, grad_shared, grad_step, grad_conv_v, grad_conv_vb, grad_conv_s, grad_conv_sb, grad_step_bias, grad_decay, grad_skip, grad_gain_gate, grad_out))

def reference(hidden_in, cotangent, norm_gain, gate_proj, value_proj, shared_proj, step_proj, conv_value, conv_value_bias, conv_shared, conv_shared_bias, step_bias, decay_log, skip_scale, gate_gain, out_proj):
    stacked = (norm_gain, gate_proj, value_proj, shared_proj, step_proj, conv_value, conv_value_bias, conv_shared, conv_shared_bias, step_bias, decay_log, skip_scale, gate_gain, out_proj)
    outs_hidden = []
    outs_grad = []
    grad_sums = []
    for seq_index in range(SEQS):
        hidden = hidden_in[seq_index]
        stored_all = []
        for layer_index in range(LAYERS):
            hidden, stored = layer_forward(hidden, layer_slice(stacked, layer_index))
            stored_all.append(stored)
        outs_hidden.append(hidden)
        d_hidden = cotangent[seq_index]
        layer_grads = [None] * LAYERS
        for layer_index in reversed(range(LAYERS)):
            d_hidden, layer_grads[layer_index] = layer_backward(d_hidden, stored_all[layer_index], layer_slice(stacked, layer_index))
        outs_grad.append(d_hidden)
        stacked_grads = [jnp.stack([entry[i] for entry in layer_grads]) for i in range(14)]
        if seq_index == 0:
            grad_sums = stacked_grads
        else:
            grad_sums = [left + right for left, right in zip(grad_sums, stacked_grads)]
    return (jnp.stack(outs_hidden), jnp.stack(outs_grad), grad_sums[0], grad_sums[1], grad_sums[2], grad_sums[3], grad_sums[4], grad_sums[5], grad_sums[6], grad_sums[7], grad_sums[8], grad_sums[9], grad_sums[10], grad_sums[11], grad_sums[12], grad_sums[13])
```

```python
import functools

import jax
import jax.numpy as jnp
from jax import lax
from jax.experimental import pallas as pl
from jax.experimental.pallas import tpu as pltpu
from jax.sharding import PartitionSpec as P

epsilon = 1e-05
highest = lax.Precision.HIGHEST
MESH_ID = pl.DeviceIdType.MESH
VMEM = pl.BlockSpec(memory_space=pltpu.VMEM)


def flat_index(axes):
    index = 0
    for axis, size in axes:
        index = index * size + lax.axis_index(axis)
    return index


def device_of(axes, flat):
    if len(axes) == 1:
        return {axes[0][0]: flat}
    (outer, _), (inner, size) = axes
    return {outer: flat // size, inner: flat % size}


def greet(devices):
    barrier = pltpu.get_barrier_semaphore()
    for device in devices:
        pl.semaphore_signal(barrier, inc=1, device_id=device, device_id_type=MESH_ID)
    return barrier


def all_reduce_kernel(axes, count, x_ref, o_ref, recv, send1, recv1, send2, recv2):
    me = flat_index(axes)
    peers = [lax.rem(me + d, count) for d in range(1, count)]
    barrier = greet([device_of(axes, peer) for peer in peers])
    pl.semaphore_wait(barrier, count - 1)
    first = []
    for d, peer in enumerate(peers):
        copy = pltpu.make_async_remote_copy(
            src_ref=x_ref.at[peer],
            dst_ref=recv.at[d],
            send_sem=send1.at[d],
            recv_sem=recv1.at[d],
            device_id=device_of(axes, peer),
            device_id_type=MESH_ID,
        )
        copy.start()
        first.append(copy)
    total = x_ref[me]
    for d, copy in enumerate(first):
        copy.wait_recv()
        total = total + recv[d]
    o_ref[me] = total
    second = []
    for d, peer in enumerate(peers):
        copy = pltpu.make_async_remote_copy(
            src_ref=o_ref.at[me],
            dst_ref=o_ref.at[me],
            send_sem=send2.at[d],
            recv_sem=recv2.at[d],
            device_id=device_of(axes, peer),
            device_id_type=MESH_ID,
        )
        copy.start()
        second.append(copy)
    for copy in first:
        copy.wait_send()
    for copy in second:
        copy.wait()


def all_reduce(x, axes, collective_id):
    axes = [(axis, lax.axis_size(axis)) for axis in axes]
    count = 1
    for _, size in axes:
        count *= size
    rows, width = x.shape
    part = (rows // count, width)
    out = pl.pallas_call(
        functools.partial(all_reduce_kernel, axes, count),
        out_shape=jax.ShapeDtypeStruct((count,) + part, jnp.float32),
        in_specs=[VMEM],
        out_specs=VMEM,
        scratch_shapes=[pltpu.VMEM((count - 1,) + part, jnp.float32)]
        + [pltpu.SemaphoreType.DMA((count - 1,))] * 4,
        compiler_params=pltpu.CompilerParams(
            collective_id=collective_id, has_side_effects=True
        ),
    )(x.reshape((count,) + part))
    return out.reshape(rows, width)


def placed(shapes, rows):
    pieces, at = [], 0
    for number, (height, _) in enumerate(shapes):
        begin = 0
        while begin < height:
            peer, inside = at // rows, at % rows
            take = min(height - begin, rows - inside)
            pieces.append((number, begin, take, peer, inside))
            begin, at = begin + take, at + take
    return pieces


def reduce_many_kernel(axes, count, shapes, outs, *refs):
    number = len(shapes)
    inputs, refs = refs[:number], refs[number:]
    outputs, refs = refs[: len(outs)], refs[len(outs) :]
    packed, total, *rest = refs
    pieces = placed(shapes, packed.shape[1])
    packed[...] = jnp.zeros_like(packed)
    for i, begin, take, peer, inside in pieces:
        packed[peer, inside : inside + take, : shapes[i][1]] = inputs[i][begin : begin + take, :]
    all_reduce_kernel(axes, count, packed, total, *rest)
    target = {}
    for o, members in enumerate(outs):
        for layer, i in enumerate(members):
            target[i] = (o, layer)
    for i, begin, take, peer, inside in pieces:
        o, layer = target[i]
        value = total[peer, inside : inside + take, : shapes[i][1]]
        if len(outputs[o].shape) == 3:
            outputs[o][layer, begin : begin + take, :] = value
        else:
            outputs[o][layer : layer + 1, :] = value


def reduce_many(groups, axes, collective_id):
    axes = [(axis, lax.axis_size(axis)) for axis in axes]
    count = 1
    for _, size in axes:
        count *= size
    arrays, outs, out_shapes = [], [], []
    for group in groups:
        outs.append(list(range(len(arrays), len(arrays) + len(group))))
        arrays += [array.reshape((-1, array.shape[-1])) for array in group]
        out_shapes.append(jax.ShapeDtypeStruct((len(group),) + group[0].shape, jnp.float32))
    shapes = [array.shape for array in arrays]
    height = sum(shape[0] for shape in shapes)
    rows = -(-height // (8 * count)) * 8
    part = (rows, -(-max(shape[1] for shape in shapes) // 128) * 128)
    return pl.pallas_call(
        functools.partial(reduce_many_kernel, axes, count, shapes, outs),
        out_shape=out_shapes,
        in_specs=[VMEM] * len(arrays),
        out_specs=[VMEM] * len(out_shapes),
        scratch_shapes=[pltpu.VMEM((count,) + part, jnp.float32)] * 2
        + [pltpu.VMEM((count - 1,) + part, jnp.float32)]
        + [pltpu.SemaphoreType.DMA((count - 1,))] * 4,
        compiler_params=pltpu.CompilerParams(
            collective_id=collective_id, has_side_effects=True
        ),
    )(*arrays)


def chain_kernel(count, step, decay_ref, end_ref, start_ref, held, send, recv):
    me = lax.axis_index("seq")
    first, last = (0, count - 1) if step == 1 else (count - 1, 0)
    after = lax.rem(me + step + count, count)
    before = lax.rem(me - step + count, count)
    barrier = pltpu.get_barrier_semaphore()

    @pl.when(me != first)
    def _():
        pl.semaphore_signal(barrier, inc=1, device_id={"seq": before}, device_id_type=MESH_ID)

    @pl.when(me != last)
    def _():
        pl.semaphore_wait(barrier, 1)

    copies = [
        pltpu.make_async_remote_copy(
            src_ref=held.at[h],
            dst_ref=start_ref.at[h],
            send_sem=send.at[h],
            recv_sem=recv.at[h],
            device_id={"seq": after},
            device_id_type=MESH_ID,
        )
        for h in range(end_ref.shape[0])
    ]
    for h, copy in enumerate(copies):

        @pl.when(me == first)
        def _():
            start_ref[h] = jnp.zeros_like(start_ref[h])
            held[h] = end_ref[h]

        @pl.when(me != first)
        def _():
            copy.wait_recv()
            held[h] = decay_ref[h] * start_ref[h] + end_ref[h]

        @pl.when(me != last)
        def _():
            copy.start()

    @pl.when(me != last)
    def _():
        for copy in copies:
            copy.wait_send()


def chain(decay, end, step, collective_id):
    count = lax.axis_size("seq")
    heads = end.shape[0]
    return pl.pallas_call(
        functools.partial(chain_kernel, count, step),
        out_shape=jax.ShapeDtypeStruct(end.shape, jnp.float32),
        in_specs=[VMEM, VMEM],
        out_specs=VMEM,
        scratch_shapes=[pltpu.VMEM(end.shape, jnp.float32)]
        + [pltpu.SemaphoreType.DMA((heads,))] * 2,
        compiler_params=pltpu.CompilerParams(
            collective_id=collective_id, has_side_effects=True
        ),
    )(jnp.broadcast_to(decay[:, None, None], (heads, 1, end.shape[2])), end)


def shift_kernel(count, step, x_ref, o_ref, send, recv):
    me = lax.axis_index("seq")
    first, last = (0, count - 1) if step == 1 else (count - 1, 0)
    after = lax.rem(me + step + count, count)
    before = lax.rem(me - step + count, count)
    barrier = pltpu.get_barrier_semaphore()

    @pl.when(me != first)
    def _():
        pl.semaphore_signal(barrier, inc=1, device_id={"seq": before}, device_id_type=MESH_ID)

    copy = pltpu.make_async_remote_copy(
        src_ref=x_ref,
        dst_ref=o_ref,
        send_sem=send,
        recv_sem=recv,
        device_id={"seq": after},
        device_id_type=MESH_ID,
    )

    @pl.when(me != last)
    def _():
        pl.semaphore_wait(barrier, 1)
        copy.start()

    @pl.when(me == first)
    def _():
        o_ref[...] = jnp.zeros_like(o_ref)

    @pl.when(me != first)
    def _():
        copy.wait_recv()

    @pl.when(me != last)
    def _():
        copy.wait_send()


def shift(x, step, collective_id):
    return pl.pallas_call(
        functools.partial(shift_kernel, lax.axis_size("seq"), step),
        out_shape=jax.ShapeDtypeStruct(x.shape, jnp.float32),
        in_specs=[VMEM],
        out_specs=VMEM,
        scratch_shapes=[pltpu.SemaphoreType.DMA] * 2,
        compiler_params=pltpu.CompilerParams(
            collective_id=collective_id, has_side_effects=True
        ),
    )(x)


def scatter_kernel(count, pairs, number, cuts, *refs):
    inputs, refs = refs[:number], refs[number:]
    outputs, refs = refs[: len(cuts)], refs[len(cuts) :]
    from_core, refs = refs[:number], refs[number:]
    partial, refs = refs[:number], refs[number:]
    from_left, refs = refs[:number], refs[number:]
    from_right, refs = refs[:number], refs[number:]
    core_send, core_recv, right_send, right_recv, left_send, left_recv = refs
    me, core = lax.axis_index("seq"), lax.axis_index("batch")
    others = [lax.rem(core + d, pairs) for d in range(1, pairs)]
    barrier = greet([{"batch": other} for other in others])
    right, left = lax.rem(me + 1, count), lax.rem(me + count - 1, count)

    @pl.when(me > 0)
    def _():
        pl.semaphore_signal(barrier, inc=1, device_id={"seq": left}, device_id_type=MESH_ID)

    @pl.when(me < count - 1)
    def _():
        pl.semaphore_signal(barrier, inc=1, device_id={"seq": right}, device_id_type=MESH_ID)

    edges = jnp.where(me > 0, 1, 0) + jnp.where(me < count - 1, 1, 0)
    pl.semaphore_wait(barrier, pairs - 1 + edges)

    order = []
    for k in range((count + 1) // 2):
        order.append(k)
        if count - 1 - k != k:
            order.append(count - 1 - k)
    across = {}
    for s in order:
        for i in range(number):
            for d, other in enumerate(others):
                across[i, s, d] = pltpu.make_async_remote_copy(
                    src_ref=inputs[i].at[s, other],
                    dst_ref=from_core[i].at[d, s],
                    send_sem=core_send.at[i, d, s],
                    recv_sem=core_recv.at[i, d, s],
                    device_id={"batch": other},
                    device_id_type=MESH_ID,
                )
                across[i, s, d].start()

    def along(i, s, buffer, sends, recvs, target):
        return pltpu.make_async_remote_copy(
            src_ref=partial[i].at[s],
            dst_ref=buffer[i].at[s],
            send_sem=sends.at[i, s],
            recv_sem=recvs.at[i, s],
            device_id={"seq": target},
            device_id_type=MESH_ID,
        )

    rightward = {
        (i, s): along(i, s, from_left, right_send, right_recv, right)
        for i in range(number)
        for s in range(1, count)
    }
    leftward = {
        (i, s): along(i, s, from_right, left_send, left_recv, left)
        for i in range(number)
        for s in range(count - 1)
    }
    done = set()

    def prepare(i, s):
        if (i, s) in done:
            return
        done.add((i, s))
        total = inputs[i][s, core]
        for d in range(len(others)):
            across[i, s, d].wait_recv()
            total = total + from_core[i][d, s]
        partial[i][s] = total

    def go_right(i, s, when):
        @pl.when(jnp.logical_and(when, me < s))
        def _():
            @pl.when(me > 0)
            def _():
                rightward[i, s].wait_recv()
                partial[i][s] = partial[i][s] + from_left[i][s]

            rightward[i, s].start()

    def go_left(i, s):
        @pl.when(me > s)
        def _():
            @pl.when(me < count - 1)
            def _():
                leftward[i, s].wait_recv()
                partial[i][s] = partial[i][s] + from_right[i][s]

            leftward[i, s].start()

    early = 2 * me < count
    for k in range(count - 1):
        for i in range(number):
            prepare(i, count - 1 - k)
            prepare(i, k)
            go_right(i, count - 1 - k, early)
            go_left(i, k)
            go_right(i, count - 1 - k, jnp.logical_not(early))
    for s in range(count):
        for i in range(number):
            prepare(i, s)

    for i in range(number):
        for s in range(count):

            @pl.when(me == s)
            def _():
                total = partial[i][s]

                def store(value):
                    for o, (kind, low, high) in enumerate(cuts):
                        if i % 2 == kind:
                            outputs[o][i // 2] = value[:, low:high]

                if s > 0:
                    rightward[i, s].wait_recv()
                    total = total + from_left[i][s]
                if s < count - 1:
                    leftward[i, s].wait_recv()
                    total = total + from_right[i][s]
                store(total)

    for copy in across.values():
        copy.wait_send()
    for (i, s), copy in rightward.items():

        @pl.when(me < s)
        def _():
            copy.wait_send()

    for (i, s), copy in leftward.items():

        @pl.when(me > s)
        def _():
            copy.wait_send()


def scatter_sum(grads, cuts, collective_id):
    count, pairs = lax.axis_size("seq"), lax.axis_size("batch")
    number = len(grads)
    parts = [(grad.shape[0] // (count * pairs), grad.shape[1]) for grad in grads]
    return pl.pallas_call(
        functools.partial(scatter_kernel, count, pairs, number, cuts),
        out_shape=[
            jax.ShapeDtypeStruct((number // 2, parts[kind][0], high - low), jnp.float32)
            for kind, low, high in cuts
        ],
        in_specs=[VMEM] * number,
        out_specs=[VMEM] * len(cuts),
        scratch_shapes=[pltpu.VMEM((pairs - 1, count) + part, jnp.float32) for part in parts]
        + [pltpu.VMEM((count,) + part, jnp.float32) for part in parts] * 3
        + [pltpu.SemaphoreType.DMA((number, pairs - 1, count))] * 2
        + [pltpu.SemaphoreType.DMA((number, count))] * 4,
        compiler_params=pltpu.CompilerParams(
            collective_id=collective_id, has_side_effects=True, vmem_limit_bytes=60 * 1024 * 1024
        ),
    )(*[grad.reshape((count, pairs) + part) for grad, part in zip(grads, parts)])


def silu_slope(argument):
    sigmoid_value = jax.nn.sigmoid(argument)
    return sigmoid_value * (1.0 + argument * (1.0 - sigmoid_value))


def norm_input(hidden, norm_gain):
    return (
        hidden * lax.rsqrt(jnp.mean(hidden * hidden, axis=-1, keepdims=True) + epsilon) * norm_gain
    )


def spread(per_head, width):
    heads = per_head.shape[-1]
    owner = jnp.arange(width) // (width // heads)
    table = (jnp.arange(heads)[:, None] == owner[None, :]).astype(jnp.float32)
    return jnp.dot(per_head, table, precision=highest)


def ssd_front(
    ext_value,
    ext_shared,
    conv_value,
    conv_value_bias,
    conv_shared,
    conv_shared_bias,
    step_raw,
    step_bias,
    decay_log,
):
    row_count, head_count = step_raw.shape
    value_conv, shared_conv = conv_value_bias, conv_shared_bias
    for k in range(conv_value.shape[0]):
        value_conv = value_conv + conv_value[k] * ext_value[k : k + row_count]
        shared_conv = shared_conv + conv_shared[k] * ext_shared[k : k + row_count]
    values = jax.nn.silu(value_conv)
    shared_act = jax.nn.silu(shared_conv)
    state_width = shared_act.shape[1] // 2
    b_mat = shared_act[:, :state_width]
    c_mat = shared_act[:, state_width:]
    step = jax.nn.softplus(step_raw + step_bias)
    rate = -jnp.exp(decay_log) * step
    positions = jnp.arange(row_count)
    causal = (positions[:, None] >= positions[None, :]).astype(jnp.float32)
    cum = jnp.dot(causal, rate, precision=highest)
    to_end = jnp.exp(cum[-1:] - cum)
    weighted = values * spread(to_end * step, values.shape[1])
    end_state = lax.dot_general(weighted, b_mat, (((0,), (0,)), ((), ())))
    return values, b_mat, c_mat, step, cum, end_state, jnp.exp(cum[-1])


def ssd_output(values, b_mat, c_mat, step, cum, skip_scale, start_state):
    row_count, head_count = step.shape
    width = values.shape[1]
    scores = lax.dot_general(c_mat, b_mat, (((1,), (1,)), ((), ())))
    positions = jnp.arange(row_count)
    causal = positions[:, None] >= positions[None, :]
    cum_heads = cum.T
    gap = cum_heads[:, :, None] - cum_heads[:, None, :]
    weights = jnp.where(causal, jnp.exp(jnp.where(causal, gap, 0.0)), 0.0)
    mixing = scores[None] * weights * step.T[:, None, :]
    within = jnp.einsum("hts,shp->thp", mixing, values.reshape(row_count, head_count, -1))
    carried = lax.dot_general(c_mat, start_state, (((1,), (1,)), ((), ())))
    carried = carried * spread(jnp.exp(cum), width)
    skipped = spread(skip_scale[None], width) * values
    return within.reshape(row_count, width) + carried + skipped


def layer_forward(hidden, weights):
    (norm_gain, wide_proj, conv_v, conv_vb, conv_s, conv_sb, step_bias, decay_log) = weights[:8]
    (skip_scale, gate_gain, out_proj) = weights[8:]
    inner, shared = conv_v.shape[1], conv_s.shape[1]
    heads = step_bias.shape[0]
    normed_b = norm_input(hidden, norm_gain).astype(jnp.bfloat16)
    wide = jnp.dot(normed_b, wide_proj, preferred_element_type=jnp.float32)
    gate_pre = wide[:, :inner]
    mixed = wide[:, inner : 2 * inner + shared]
    step_raw = wide[:, 2 * inner + shared :]
    rim = conv_v.shape[0] - 1
    before = shift(mixed[-8:], 1, 1)[-rim:]
    ext = jnp.concatenate([before, mixed], axis=0)
    front_out, front_pull = jax.vjp(
        ssd_front,
        ext[:, :inner],
        ext[:, inner:],
        conv_v,
        conv_vb,
        conv_s,
        conv_sb,
        step_raw,
        step_bias,
        decay_log,
    )
    values, b_mat, c_mat, step, cum, end_state, decay_total = front_out
    states = (heads, inner // heads, end_state.shape[1])
    start_state = chain(decay_total, end_state.reshape(states), 1, 2).reshape(end_state.shape)
    mixer_out, output_pull = jax.vjp(
        ssd_output, values, b_mat, c_mat, step, cum, skip_scale, start_state
    )
    gated = mixer_out * jax.nn.silu(gate_pre)
    branch = jnp.dot(
        (gated * gate_gain).astype(jnp.bfloat16), out_proj, preferred_element_type=jnp.float32
    )
    square = jnp.sum(gated * gated, axis=-1, keepdims=True)
    square = jnp.broadcast_to(square, (square.shape[0], 128))
    width = branch.shape[1]
    both = all_reduce(jnp.concatenate([branch, square], axis=1), ["head"], 3)
    branch = both[:, :width]
    inner_width = inner * lax.axis_size("head")
    inv_rms = lax.rsqrt(both[:, width : width + 1] / inner_width + epsilon)
    stored = (
        normed_b,
        gate_pre,
        front_pull,
        output_pull,
        mixer_out,
        gated,
        inv_rms,
        branch,
        hidden,
        start_state,
        decay_total,
    )
    return hidden + branch * inv_rms, stored


def layer_backward(d_hidden, stored, weights):
    (norm_gain, wide_proj, conv_v, conv_vb, conv_s, conv_sb, step_bias, decay_log) = weights[:8]
    (skip_scale, gate_gain, out_proj) = weights[8:]
    (
        normed_b,
        gate_pre,
        front_pull,
        output_pull,
        mixer_out,
        gated,
        inv_rms,
        branch,
        hidden,
        start_state,
        decay_total,
    ) = stored
    inner, shared = conv_v.shape[1], conv_s.shape[1]
    heads = step_bias.shape[0]
    g_b = d_hidden.astype(jnp.bfloat16)
    d_norm = lax.dot_general(
        g_b, out_proj, (((1,), (1,)), ((), ())), preferred_element_type=jnp.float32
    )
    gated_b = (gated * inv_rms * gate_gain).astype(jnp.bfloat16)
    grad_out = lax.dot_general(
        g_b, gated_b, (((0,), (0,)), ((), ())), preferred_element_type=jnp.float32
    )
    grad_gain_gate = jnp.sum(d_norm * gated * inv_rms, axis=0)
    scaled = d_norm * gate_gain
    inner_width = inner * lax.axis_size("head")
    inner_sum = jnp.sum(g_b.astype(jnp.float32) * branch, axis=-1, keepdims=True)
    inner_dot = inner_sum / inner_width
    d_gated = inv_rms * scaled - gated * (inv_rms * inv_rms * inv_rms * inner_dot)
    d_mixer = d_gated * jax.nn.silu(gate_pre)
    d_gate_pre = d_gated * mixer_out * silu_slope(gate_pre)
    d_values, d_b, d_c, d_step, d_cum, grad_skip, d_start = output_pull(d_mixer)
    states = (heads, inner // heads, d_start.shape[1])
    d_end = chain(decay_total, d_start.reshape(states), -1, 4)
    d_total = jnp.sum(d_end * start_state.reshape(states), axis=(1, 2))
    pulled = front_pull((d_values, d_b, d_c, d_step, d_cum, d_end.reshape(d_start.shape), d_total))
    d_ext_value, d_ext_shared, g_cv, g_cvb, g_cs, g_csb, d_step_raw, g_sb, g_decay = pulled
    rim = conv_v.shape[0] - 1
    d_ext = jnp.concatenate([d_ext_value, d_ext_shared], axis=1)
    after = shift(d_ext[:8], -1, 5)
    after = jnp.concatenate([jnp.zeros_like(d_ext[2 * rim :]), after[:rim]], axis=0)
    d_mixed = d_ext[rim:] + after
    step_b = d_step_raw.astype(jnp.bfloat16)
    projected_b = jnp.concatenate(
        [d_gate_pre.astype(jnp.bfloat16), d_mixed.astype(jnp.bfloat16)], axis=1
    )
    d_wide = jnp.concatenate([projected_b, step_b], axis=1)
    partial_normed = lax.dot_general(
        d_wide, wide_proj, (((1,), (1,)), ((), ())), preferred_element_type=jnp.float32
    )
    d_normed = all_reduce(partial_normed, ["head"], 6)
    grad_wide = lax.dot_general(
        normed_b, projected_b, (((0,), (0,)), ((), ())), preferred_element_type=jnp.float32
    )
    grad_step = lax.dot_general(
        step_b, normed_b, (((0,), (0,)), ((), ())), preferred_element_type=jnp.float32
    )
    _, norm_pull = jax.vjp(norm_input, hidden, norm_gain)
    d_input, grad_norm = norm_pull(d_normed)
    small = (grad_norm, g_cv, g_cvb, g_sb, g_decay, grad_skip, grad_gain_gate, grad_step, g_cs, g_csb)
    return d_hidden + d_input, (grad_wide, grad_out), small


def body(
    hidden_in,
    cotangent,
    norm_gain,
    gate_proj,
    value_proj,
    shared_proj,
    step_proj,
    conv_value,
    conv_value_bias,
    conv_shared,
    conv_shared_bias,
    step_bias,
    decay_log,
    skip_scale,
    gate_gain,
    out_proj,
):
    wide_proj = jnp.concatenate([gate_proj, value_proj, shared_proj, step_proj], axis=2)
    stacked = (
        norm_gain,
        wide_proj,
        conv_value,
        conv_value_bias,
        conv_shared,
        conv_shared_bias,
        step_bias,
        decay_log,
        skip_scale,
        gate_gain,
        out_proj,
    )
    layer_total = norm_gain.shape[0]
    layers = [tuple(tensor[at] for tensor in stacked) for at in range(layer_total)]
    hidden = hidden_in[0]
    stored_all = []
    for weights in layers:
        hidden, stored = layer_forward(hidden, weights)
        stored_all.append(stored)
    d_hidden = cotangent[0]
    large, small = [None] * layer_total, [None] * layer_total
    for at in reversed(range(layer_total)):
        d_hidden, large[at], small[at] = layer_backward(d_hidden, stored_all[at], layers[at])
    inner = conv_value.shape[2]
    count, pairs = lax.axis_size("seq"), lax.axis_size("batch")
    shared = conv_shared.shape[2]
    cuts = (
        (0, 0, inner),
        (0, inner, 2 * inner),
        (0, 2 * inner, 2 * inner + shared),
        (1, 0, inner),
    )
    gate_sum, value_sum, shared_part, out_sum = scatter_sum(
        [grad for at in range(layer_total) for grad in large[at]], cuts, 7
    )
    out_sum = jnp.swapaxes(out_sum, 1, 2)
    groups = [[small[at][i] for at in range(layer_total)] for i in range(10)]
    totals = reduce_many(groups, ["seq", "batch"], 8)
    over_heads = [
        [group[at] for at in range(layer_total)] for group in (shared_part, totals[8], totals[9])
    ]
    shared_sum, conv_shared_sum, conv_bias_sum = reduce_many(over_heads, ["head"], 9)
    mine = gate_sum.shape[1]
    at = lax.axis_index("seq") * pairs + lax.axis_index("batch")
    step_sum = jnp.swapaxes(lax.dynamic_slice_in_dim(totals[7], at * mine, mine, axis=2), 1, 2)
    return (
        hidden[None],
        d_hidden[None],
        totals[0],
        gate_sum,
        value_sum,
        shared_sum,
        step_sum,
        totals[1],
        totals[2],
        conv_shared_sum,
        conv_bias_sum,
        totals[3],
        totals[4],
        totals[5],
        totals[6],
        out_sum,
    )


def solution(mesh):
    return jax.shard_map(
        body,
        mesh=mesh,
        in_specs=(
            P("batch", "seq", None),
            P("batch", "seq", None),
            P(),
            P(None, None, "head"),
            P(None, None, "head"),
            P(),
            P(None, None, "head"),
            P(None, None, "head"),
            P(None, "head"),
            P(),
            P(),
            P(None, "head"),
            P(None, "head"),
            P(None, "head"),
            P(None, "head"),
            P(None, "head", None),
        ),
        out_specs=(
            P("batch", "seq", None),
            P("batch", "seq", None),
            P(),
            P(None, ("seq", "batch"), "head"),
            P(None, ("seq", "batch"), "head"),
            P(None, ("seq", "batch"), None),
            P(None, ("seq", "batch"), "head"),
            P(None, None, "head"),
            P(None, "head"),
            P(),
            P(),
            P(None, "head"),
            P(None, "head"),
            P(None, "head"),
            P(None, "head"),
            P(None, "head", ("seq", "batch")),
        ),
        check_vma=False,
    )
```
